32 devices in a mesh: grp: 4 (over y, x), col: 8 (over z, core).
Axes of the slice: x: 2, y: 2, z: 4, core: 2. Of those that a mesh axis runs over, the one named last changes fastest.
Arguments:
- start_block: float32 [16, 8192], P(None, ('grp', 'col')), may hold values from -6 to 6
- tile_values: float32 [4, 8, 32, 256, 256], P('grp', 'col'), may hold values from 0 to 1, as said below
- tile_row: int32 [4, 8, 32], P('grp', 'col'), may hold values from 0 to 31, as said below
- tile_col: int32 [4, 8, 32], P('grp', 'col'), may hold values from 0 to 31, as said below
- tile_count: int32 [4, 8], P('grp', 'col'), may hold values from 8 to 32, as said below
Outputs:
- basis: float32 [5, 16, 8192], P(None, None, ('grp', 'col'))
- projections: float32 [4, 4, 16, 16], replicated
- factors: float32 [5, 16, 16], replicated
The draws below stay inside these ranges and needn't reach their ends.
Inputs may be any that keep to these rules, and one draw needn't show every extreme that they name: `tile_row`: A tile of the device at grp index g lies in tile rows g * 8 * 1 to (g + 1) * 8 - 1. `tile_col`: A tile column t of the device at col index c has (t) % 8 == c. Coordinate pairs may repeat; repeated tiles add. The live tiles of a device are its first tile_count slots; some device has all 32 slots live. `tile_values`: entries are nonnegative.
All inputs are finite; a program needn't handle non-finite values.
Results may differ from the reference program's by a relative error of at most 0.0003.
Values sent between devices are 32-bit elements; how exact they have to be, the bound alone decides.
A program may use at most 64 MiB of HBM per device.

```python
import math
import jax
import jax.numpy as jnp
from jax import lax

TILE = 256
BLOCK = 16
ITERS = 4
ROW_TILES = 1
SLOTS = 32
NODES = 8192
N_GRP = 4
N_COL = 8


def draw_tile_row(key, part):
    offsets = jax.random.randint(jax.random.fold_in(key, 11), (N_GRP, N_COL, SLOTS), 0, N_COL * ROW_TILES, dtype=jnp.int32)
    groups = jnp.arange(N_GRP, dtype=jnp.int32)[:, None, None]
    return groups * (N_COL * ROW_TILES) + offsets


def draw_tile_col(key, part):
    group_pick = jax.random.randint(jax.random.fold_in(key, 21), (N_GRP, N_COL, SLOTS), 0, N_GRP, dtype=jnp.int32)
    within = jax.random.randint(jax.random.fold_in(key, 22), (N_GRP, N_COL, SLOTS), 0, ROW_TILES, dtype=jnp.int32)
    columns = jnp.arange(N_COL, dtype=jnp.int32)[None, :, None]
    return (group_pick * N_COL + columns) * ROW_TILES + within


def draw_tile_count(key, part):
    counts = jax.random.randint(jax.random.fold_in(key, 31), (N_GRP, N_COL), max(1, SLOTS // 4), SLOTS + 1, dtype=jnp.int32)
    chosen = jax.random.randint(jax.random.fold_in(key, 32), (), 0, N_GRP * N_COL, dtype=jnp.int32)
    flat_index = jnp.arange(N_GRP * N_COL, dtype=jnp.int32).reshape(N_GRP, N_COL)
    return jnp.where(flat_index == chosen, SLOTS, counts).astype(jnp.int32)


def draw_tile_values(key, part):
    array_shape = (N_GRP, N_COL, SLOTS, TILE, TILE)
    lowest = 0.1
    entries = jax.random.uniform(jax.random.fold_in(key, 41), array_shape, jnp.float32)
    row_scale = jnp.exp(jax.random.uniform(jax.random.fold_in(key, 42), (N_GRP, N_COL, SLOTS, TILE, 1), jnp.float32, math.log(lowest), 0.0))
    col_scale = jnp.exp(jax.random.uniform(jax.random.fold_in(key, 43), (N_GRP, N_COL, SLOTS, 1, TILE), jnp.float32, math.log(lowest), 0.0))
    return entries * row_scale * col_scale * (20.0 * ROW_TILES / (SLOTS * TILE))


def block_scale(stream_key, shape, cuts, low, largest):
    level = 1.0
    for axis_at, blocks in cuts:
        draws = jax.random.uniform(jax.random.fold_in(jax.random.fold_in(stream_key, 6), axis_at), (blocks,), jnp.float32, low / len(cuts), largest / len(cuts))
        level = level * jnp.repeat(jnp.exp(draws), shape[axis_at] // blocks).reshape((-1,) + (1,) * (len(shape) - 1 - axis_at))
    return level


def noise(key, dims, deviation, limit, cuts=(), held_as=jnp.bfloat16):
    drawn = deviation * jax.random.normal(key, dims, jnp.float32)
    if cuts:
        drawn = drawn * block_scale(key, dims, cuts, -0.22, 0.18)
    return jnp.clip(drawn, -limit, limit).astype(held_as)


def setup_inputs(seed: int = 0) -> dict:
    splits = jax.random.split(jax.random.key(seed), 6)
    start_block = noise(splits[0], (BLOCK, NODES), 1.0, 6.0, ((1, 32),), jnp.float32)
    tile_values = draw_tile_values(jax.random.fold_in(splits[5], 71), 0)
    tile_row = draw_tile_row(jax.random.fold_in(splits[5], 71), 0)
    tile_col = draw_tile_col(jax.random.fold_in(splits[5], 71), 0)
    tile_count = draw_tile_count(jax.random.fold_in(splits[5], 71), 0)
    return {"start_block": start_block, "tile_values": tile_values, "tile_row": tile_row, "tile_col": tile_col, "tile_count": tile_count}


highest = lax.Precision.HIGHEST

def apply_weights(vector, flat_tiles, flat_rows, flat_cols, flat_live):

    def visit_tile(running, scan_item):
        tile_block, row_tile, col_tile, weight = scan_item
        row_start = (row_tile * TILE).astype(jnp.int32)
        col_start = (col_tile * TILE).astype(jnp.int32)
        col_piece = lax.dynamic_slice_in_dim(vector, col_start, TILE, 1)
        row_piece = lax.dynamic_slice_in_dim(vector, row_start, TILE, 1)
        into_rows = jnp.dot(col_piece, tile_block.T, precision=highest) * weight
        into_cols = jnp.dot(row_piece, tile_block, precision=highest) * weight
        current = lax.dynamic_slice_in_dim(running, row_start, TILE, 1)
        running = lax.dynamic_update_slice_in_dim(running, current + into_rows, row_start, 1)
        current = lax.dynamic_slice_in_dim(running, col_start, TILE, 1)
        running = lax.dynamic_update_slice_in_dim(running, current + into_cols, col_start, 1)
        return (running, None)
    initial = jnp.zeros(vector.shape, jnp.float32)
    result, unused = lax.scan(visit_tile, initial, (flat_tiles, flat_rows, flat_cols, flat_live))
    return result

def orthonormal(block_rows):
    gram_now = jnp.dot(block_rows, block_rows.T, precision=highest) / NODES
    factor = jnp.linalg.cholesky(gram_now)
    solved = jax.scipy.linalg.solve_triangular(factor, block_rows, lower=True)
    return (solved, factor)

def reference(start_block, tile_values, tile_row, tile_col, tile_count):
    flat_tiles = tile_values.reshape(-1, TILE, TILE)
    flat_rows = tile_row.reshape(-1).astype(jnp.int32)
    flat_cols = tile_col.reshape(-1).astype(jnp.int32)
    live_mask = jnp.arange(SLOTS, dtype=jnp.int32)[None, None, :] < tile_count[:, :, None]
    flat_live = live_mask.reshape(-1).astype(jnp.float32)
    ones_row = jnp.ones((1, NODES), jnp.float32)
    degree = apply_weights(ones_row, flat_tiles, flat_rows, flat_cols, flat_live)

    def laplace(vector):
        return degree * vector - apply_weights(vector, flat_tiles, flat_rows, flat_cols, flat_live)
    first_block, factor = orthonormal(start_block)
    basis_list = [first_block]
    factor_list = [factor]
    projections = jnp.zeros((ITERS, ITERS, BLOCK, BLOCK), jnp.float32)
    for step_index in range(ITERS):
        applied = laplace(basis_list[-1])
        stacked = jnp.stack(basis_list)
        coeffs = jnp.einsum('an,jbn->jab', applied, stacked, precision=highest) / NODES
        applied = applied - jnp.einsum('jab,jbn->an', coeffs, stacked, precision=highest)
        next_block, factor = orthonormal(applied)
        basis_list.append(next_block)
        factor_list.append(factor)
        projections = projections.at[step_index, :step_index + 1].set(coeffs)
    return (jnp.stack(basis_list), projections, jnp.stack(factor_list))
```

```python
import functools

import jax
import jax.numpy as jnp
from jax import lax
from jax.experimental import pallas as pl
from jax.experimental.pallas import tpu as pltpu
from jax.sharding import PartitionSpec as P

ITERS = 4
HIGHEST = lax.Precision.HIGHEST
MESH = pl.DeviceIdType.MESH
F32 = jnp.float32
BF16 = jnp.bfloat16
LANES = 128


def dot_nt(left, right, precision=None):
    dims = (((1,), (1,)), ((), ()))
    return lax.dot_general(left, right, dims, precision=precision, preferred_element_type=F32)


def dot_nn(left, right, precision=None):
    dims = (((1,), (0,)), ((), ()))
    return lax.dot_general(left, right, dims, precision=precision, preferred_element_type=F32)


def split_two(value):
    high = value.astype(BF16)
    low = (value - high.astype(F32)).astype(BF16)
    return high, low


def factorize(gram):
    width = gram.shape[0]
    row = lax.broadcasted_iota(jnp.int32, gram.shape, 0)
    lane = lax.broadcasted_iota(jnp.int32, gram.shape, 1)
    unit = jnp.where(lane == row + width, 1.0, 0.0).astype(F32)
    work = jnp.where(lane < width, gram, unit)
    for j in range(width):
        column = jnp.broadcast_to(work[:, j : j + 1], work.shape)
        pivot_row = jnp.broadcast_to(work[j : j + 1, :], work.shape)
        pivot = jnp.broadcast_to(column[j : j + 1, :], work.shape)
        scale = jnp.where(row > j, column / pivot, 0.0)
        work = work - scale * pivot_row
    diagonal = jnp.sum(jnp.where(lane == row, work, 0.0), axis=1, keepdims=True)
    work = work / jnp.sqrt(diagonal)
    upper = jnp.where((lane < width) & (lane >= row), work, 0.0)
    identity = jnp.where(lane == row, 1.0, 0.0).astype(F32)
    factor = dot_nt(identity, jnp.concatenate([upper] * (LANES // width), axis=0), HIGHEST)
    return factor[:, :width], work[:, width : 2 * width]


def kernel(
    grp_size, col_size, node_total,
    start_ref, tiles_ref, row_ref, col_ref, count_ref,
    basis_ref, proj_ref, factors_ref,
    raw, high, low, q_ref, row_panel, col_panel, row_split, col_split,
    acc_row, acc_col, got_row, got_col, one_col, one_grp, two_col, two_grp,
    tile_sem, gather_row_sem, gather_col_sem, scatter_row_sem, scatter_col_sem,
    one_col_sem, one_grp_sem, two_col_sem, two_grp_sem,
):
    grp = lax.axis_index("grp")
    col = lax.axis_index("col")
    slots, tile_size = raw.shape[0], raw.shape[1]
    width = start_ref.shape[0]
    group = 4 if slots % 4 == 0 else 1

    def load_tile(s):
        return pltpu.make_async_copy(tiles_ref.at[s], raw.at[s], tile_sem.at[s])

    def start_load(s, carry):
        load_tile(s).start()
        return carry

    lax.fori_loop(0, slots, start_load, 0)

    barrier = pltpu.get_barrier_semaphore()

    def greet_col(d, carry):
        pl.semaphore_signal(
            barrier, inc=1, device_id=(grp, lax.rem(col + d, col_size)), device_id_type=MESH
        )
        return carry

    def greet_grp(d, carry):
        pl.semaphore_signal(
            barrier, inc=1, device_id=(lax.rem(grp + d, grp_size), col), device_id_type=MESH
        )
        return carry

    lax.fori_loop(1, col_size, greet_col, 0)
    lax.fori_loop(1, grp_size, greet_grp, 0)

    def exchange(axis, source, target, sems, start):
        size = col_size if axis == "col" else grp_size
        me = col if axis == "col" else grp

        def visit(d, carry):
            peer = lax.rem(me + d, size)
            copy = pltpu.make_async_remote_copy(
                src_ref=source(peer),
                dst_ref=target,
                send_sem=sems.at[0, d],
                recv_sem=sems.at[1, d],
                device_id=(grp, peer) if axis == "col" else (peer, col),
                device_id_type=MESH,
            )
            if start:
                copy.start()
            else:
                copy.wait()
            return carry

        lax.fori_loop(1, size, visit, 0, unroll=size <= 8)

    def reduce_start(part, col_buf, col_sems):
        col_buf[col] = part
        exchange("col", lambda peer: col_buf.at[col], col_buf.at[col], col_sems, True)

    def reduce_finish(col_buf, grp_buf, col_sems, grp_sems):
        exchange("col", lambda peer: col_buf.at[col], col_buf.at[col], col_sems, False)
        grp_buf[grp] = jnp.sum(col_buf[...], axis=0)
        exchange("grp", lambda peer: grp_buf.at[grp], grp_buf.at[grp], grp_sems, True)
        exchange("grp", lambda peer: grp_buf.at[grp], grp_buf.at[grp], grp_sems, False)
        return jnp.sum(grp_buf[...], axis=0) / node_total

    def gram_part(block):
        return dot_nt(block, jnp.concatenate([block] * (LANES // width), axis=0), HIGHEST)

    def scatter(start):
        exchange("col", lambda peer: acc_row.at[peer], got_row.at[col], scatter_row_sem, start)
        exchange("grp", lambda peer: acc_col.at[peer], got_col.at[grp], scatter_col_sem, start)

    def scatter_total():
        got_row[col] = acc_row[col]
        got_col[grp] = acc_col[grp]
        return jnp.sum(got_row[...], axis=0) + jnp.sum(got_col[...], axis=0)

    def add_tiles(pieces_of):
        acc_row[...] = jnp.zeros_like(acc_row)
        acc_col[...] = jnp.zeros_like(acc_col)

        def visit(n, carry):
            rows, cols, into_rows, into_cols, lives = [], [], [], [], []
            for u in range(group):
                s = n * group + u
                r = jnp.clip(row_ref[s] - grp * col_size, 0, col_size - 1)
                c = jnp.clip(lax.div(col_ref[s], col_size), 0, grp_size - 1)
                into_row, into_col = pieces_of(s, r, c)
                rows.append(r)
                cols.append(c)
                lives.append(jnp.where(s < count_ref[0], 1.0, 0.0).astype(F32))
                into_rows.append(into_row)
                into_cols.append(into_col)
            for size, acc, places, pieces in (
                (col_size, acc_row, rows, into_rows),
                (grp_size, acc_col, cols, into_cols),
            ):
                for place in range(size):
                    total = acc[place]
                    for u in range(group):
                        total = total + jnp.where(places[u] == place, lives[u], 0.0) * pieces[u]
                    acc[place] = total
            return carry

        lax.fori_loop(0, slots // group, visit, 0)

    ones = jnp.ones((width, tile_size), BF16)

    def degree_pieces(s, r, c):
        load_tile(s).wait()
        first, second = split_two(raw[s])
        high[s] = first
        low[s] = second
        into_row = dot_nt(ones, first) + dot_nt(ones, second)
        into_col = dot_nn(ones, first) + dot_nn(ones, second)
        return into_row, into_col

    def product_pieces(s, r, c):
        first, second = high[s], low[s]
        at_col, at_row = col_split[c], row_split[r]
        into_row = dot_nt(at_col, first)
        into_row = into_row[:width] + into_row[width:] + dot_nt(at_col[:width], second)
        into_col = dot_nn(at_row, first)
        into_col = into_col[:width] + into_col[width:] + dot_nn(at_row[:width], second)
        return into_row, into_col

    q_ref[...] = jnp.zeros_like(q_ref)
    proj_ref[...] = jnp.zeros_like(proj_ref)
    start_part = gram_part(start_ref[...])
    pl.semaphore_wait(barrier, col_size + grp_size - 2)
    reduce_start(start_part, two_col, two_col_sem)
    add_tiles(degree_pieces)
    scatter(True)
    gram = reduce_finish(two_col, two_grp, two_col_sem, two_grp_sem)
    factor, inverse = factorize(gram)
    factors_ref[0] = factor
    q_ref[0] = dot_nn(inverse, start_ref[...], HIGHEST)
    scatter(False)
    degree = scatter_total()

    def step(k, carry):
        exchange("col", lambda peer: q_ref.at[k], row_panel.at[col], gather_row_sem, True)
        exchange("grp", lambda peer: q_ref.at[k], col_panel.at[grp], gather_col_sem, True)
        newest = q_ref[k]
        row_panel[col] = newest
        col_panel[grp] = newest
        exchange("grp", lambda peer: q_ref.at[k], col_panel.at[grp], gather_col_sem, False)
        exchange("col", lambda peer: q_ref.at[k], row_panel.at[col], gather_row_sem, False)
        for size, panel, halves in (
            (grp_size, col_panel, col_split),
            (col_size, row_panel, row_split),
        ):
            for place in range(size):
                first, second = split_two(panel[place])
                halves[place, :width] = first
                halves[place, width:] = second
        add_tiles(product_pieces)
        scatter(True)
        scatter(False)
        applied = degree * newest - scatter_total()
        stacked = q_ref[...].reshape(-1, tile_size)
        reduce_start(dot_nt(applied, stacked, HIGHEST), one_col, one_col_sem)
        coeffs = reduce_finish(one_col, one_grp, one_col_sem, one_grp_sem)
        for j in range(ITERS):
            proj_ref[k, j] = coeffs[:, j * width : (j + 1) * width]
        residual = applied - dot_nn(coeffs, stacked, HIGHEST)
        reduce_start(gram_part(residual), two_col, two_col_sem)
        gram_now = reduce_finish(two_col, two_grp, two_col_sem, two_grp_sem)
        factor_now, inverse_now = factorize(gram_now)
        factors_ref[k + 1] = factor_now
        q_ref[k + 1] = dot_nn(inverse_now, residual, HIGHEST)
        return carry

    lax.fori_loop(0, ITERS, step, 0)
    basis_ref[...] = q_ref[: ITERS + 1]


def solution(mesh):
    grp_size, col_size = mesh.shape["grp"], mesh.shape["col"]

    def body(start_block, tile_values, tile_row, tile_col, tile_count):
        width, shard_len = start_block.shape
        slots, tile_size = tile_values.shape[2], tile_values.shape[3]
        assert shard_len == tile_size and LANES % width == 0
        places = LANES // width
        node_total = shard_len * grp_size * col_size
        vmem = pl.BlockSpec(memory_space=pltpu.VMEM)
        smem = pl.BlockSpec(memory_space=pltpu.SMEM)
        block = (width, tile_size)
        small = (width, LANES)

        def sems(size):
            return pltpu.SemaphoreType.DMA((2, size))

        return pl.pallas_call(
            functools.partial(kernel, grp_size, col_size, node_total),
            out_shape=(
                jax.ShapeDtypeStruct((ITERS + 1,) + block, F32),
                jax.ShapeDtypeStruct((ITERS, ITERS, width, width), F32),
                jax.ShapeDtypeStruct((ITERS + 1, width, width), F32),
            ),
            in_specs=[vmem, pl.BlockSpec(memory_space=pl.ANY), smem, smem, smem],
            out_specs=(vmem, vmem, vmem),
            scratch_shapes=[
                pltpu.VMEM((slots, tile_size, tile_size), F32),
                pltpu.VMEM((slots, tile_size, tile_size), BF16),
                pltpu.VMEM((slots, tile_size, tile_size), BF16),
                pltpu.VMEM((places,) + block, F32),
                pltpu.VMEM((col_size,) + block, F32),
                pltpu.VMEM((grp_size,) + block, F32),
                pltpu.VMEM((col_size, 2 * width, tile_size), BF16),
                pltpu.VMEM((grp_size, 2 * width, tile_size), BF16),
                pltpu.VMEM((col_size,) + block, F32),
                pltpu.VMEM((grp_size,) + block, F32),
                pltpu.VMEM((col_size,) + block, F32),
                pltpu.VMEM((grp_size,) + block, F32),
                pltpu.VMEM((col_size,) + small, F32),
                pltpu.VMEM((grp_size,) + small, F32),
                pltpu.VMEM((col_size,) + small, F32),
                pltpu.VMEM((grp_size,) + small, F32),
                pltpu.SemaphoreType.DMA((slots,)),
                sems(col_size), sems(grp_size), sems(col_size), sems(grp_size),
                sems(col_size), sems(grp_size), sems(col_size), sems(grp_size),
            ],
            compiler_params=pltpu.CompilerParams(
                collective_id=0, has_side_effects=True, vmem_limit_bytes=40 * 1024 * 1024
            ),
        )(
            start_block,
            tile_values.reshape(slots, tile_size, tile_size),
            tile_row.reshape(slots),
            tile_col.reshape(slots),
            tile_count.reshape(1),
        )

    in_specs = (
        P(None, ("grp", "col")),
        P("grp", "col", None, None, None),
        P("grp", "col", None),
        P("grp", "col", None),
        P("grp", "col"),
    )
    out_specs = (P(None, None, ("grp", "col")), P(), P())
    return jax.shard_map(body, mesh=mesh, in_specs=in_specs, out_specs=out_specs, check_vma=False)
```

```python
import functools

import jax
import jax.numpy as jnp
from jax import lax
from jax.experimental import pallas as pl
from jax.experimental.pallas import tpu as pltpu
from jax.sharding import PartitionSpec as P

ITERS = 4
HIGHEST = lax.Precision.HIGHEST
MESH = pl.DeviceIdType.MESH
F32 = jnp.float32
BF16 = jnp.bfloat16
LANES = 128


def dot_nt(left, right, precision=None):
    dims = (((1,), (1,)), ((), ()))
    return lax.dot_general(left, right, dims, precision=precision, preferred_element_type=F32)


def dot_nn(left, right, precision=None):
    dims = (((1,), (0,)), ((), ()))
    return lax.dot_general(left, right, dims, precision=precision, preferred_element_type=F32)


def split_two(value):
    high = value.astype(BF16)
    low = (value - high.astype(F32)).astype(BF16)
    return high, low


def factorize(gram):
    width = gram.shape[0]
    row = lax.broadcasted_iota(jnp.int32, gram.shape, 0)
    lane = lax.broadcasted_iota(jnp.int32, gram.shape, 1)
    unit = jnp.where(lane == row + width, 1.0, 0.0).astype(F32)
    work = jnp.where(lane < width, gram, unit)
    for j in range(width):
        column = jnp.broadcast_to(work[:, j : j + 1], work.shape)
        pivot_row = jnp.broadcast_to(work[j : j + 1, :], work.shape)
        pivot = jnp.broadcast_to(column[j : j + 1, :], work.shape)
        scale = jnp.where(row > j, column / pivot, 0.0)
        work = work - scale * pivot_row
    diagonal = jnp.sum(jnp.where(lane == row, work, 0.0), axis=1, keepdims=True)
    work = work / jnp.sqrt(diagonal)
    upper = jnp.where((lane < width) & (lane >= row), work, 0.0)
    identity = jnp.where(lane == row, 1.0, 0.0).astype(F32)
    factor = dot_nt(identity, jnp.concatenate([upper] * (LANES // width), axis=0), HIGHEST)
    return factor[:, :width], work[:, width : 2 * width]


def kernel(
    grp_size, col_size, node_total,
    start_ref, tiles_ref, row_ref, col_ref, count_ref,
    basis_ref, proj_ref, factors_ref,
    raw, high, low, q_ref, row_panel, col_panel, row_split, col_split,
    acc_row, acc_col, got_row, got_col, deg_row, deg_col, deg_got_row, deg_got_col,
    degree_ref, r_ref, one_col, one_grp, two_col, two_grp,
    tile_sem, gather_row_sem, gather_col_sem, scatter_row_sem, scatter_col_sem,
    deg_row_sem, deg_col_sem,
    one_col_sem, one_grp_sem, two_col_sem, two_grp_sem,
):
    grp = lax.axis_index("grp")
    col = lax.axis_index("col")
    slots, tile_size = raw.shape[0], raw.shape[1]
    width = start_ref.shape[0]
    group = 4 if slots % 4 == 0 else 1

    def load_tile(s):
        return pltpu.make_async_copy(tiles_ref.at[s], raw.at[s], tile_sem.at[s])

    def start_load(s, carry):
        load_tile(s).start()
        return carry

    lax.fori_loop(0, slots, start_load, 0)

    barrier = pltpu.get_barrier_semaphore()

    def greet_col(d, carry):
        pl.semaphore_signal(
            barrier, inc=1, device_id=(grp, lax.rem(col + d, col_size)), device_id_type=MESH
        )
        return carry

    def greet_grp(d, carry):
        pl.semaphore_signal(
            barrier, inc=1, device_id=(lax.rem(grp + d, grp_size), col), device_id_type=MESH
        )
        return carry

    lax.fori_loop(1, col_size, greet_col, 0)
    lax.fori_loop(1, grp_size, greet_grp, 0)

    def exchange(axis, source, target, sems, start):
        size = col_size if axis == "col" else grp_size
        me = col if axis == "col" else grp

        def visit(d, carry):
            peer = lax.rem(me + d, size)
            copy = pltpu.make_async_remote_copy(
                src_ref=source(peer),
                dst_ref=target,
                send_sem=sems.at[0, d],
                recv_sem=sems.at[1, d],
                device_id=(grp, peer) if axis == "col" else (peer, col),
                device_id_type=MESH,
            )
            if start:
                copy.start()
            else:
                copy.wait()
            return carry

        lax.fori_loop(1, size, visit, 0, unroll=size <= 8)

    def reduce_start(part, col_buf, col_sems):
        col_buf[col] = part
        exchange("col", lambda peer: col_buf.at[col], col_buf.at[col], col_sems, True)

    def reduce_turn(col_buf, grp_buf, col_sems, grp_sems):
        exchange("col", lambda peer: col_buf.at[col], col_buf.at[col], col_sems, False)
        grp_buf[grp] = jnp.sum(col_buf[...], axis=0)
        exchange("grp", lambda peer: grp_buf.at[grp], grp_buf.at[grp], grp_sems, True)

    def reduce_end(grp_buf, grp_sems):
        exchange("grp", lambda peer: grp_buf.at[grp], grp_buf.at[grp], grp_sems, False)
        return jnp.sum(grp_buf[...], axis=0) / node_total

    def gram_part(block):
        return dot_nt(block, jnp.concatenate([block] * (LANES // width), axis=0), HIGHEST)

    def scatter(rows, cols, row_in, col_in, row_sems, col_sems, start):
        exchange("col", lambda peer: rows.at[peer], row_in.at[col], row_sems, start)
        exchange("grp", lambda peer: cols.at[peer], col_in.at[grp], col_sems, start)

    def total_of(rows, cols, row_in, col_in):
        row_in[col] = rows[col]
        col_in[grp] = cols[grp]
        return jnp.sum(row_in[...], axis=0) + jnp.sum(col_in[...], axis=0)

    def gather(start):
        exchange("col", lambda peer: r_ref, row_panel.at[col], gather_row_sem, start)
        exchange("grp", lambda peer: r_ref, col_panel.at[grp], gather_col_sem, start)

    def add_tiles(pieces_of, sum_rows, sum_cols):
        sum_rows[...] = jnp.zeros_like(sum_rows)
        sum_cols[...] = jnp.zeros_like(sum_cols)

        def visit(n, carry):
            rows, cols, into_rows, into_cols, lives = [], [], [], [], []
            for u in range(group):
                s = n * group + u
                r = jnp.clip(row_ref[s] - grp * col_size, 0, col_size - 1)
                c = jnp.clip(lax.div(col_ref[s], col_size), 0, grp_size - 1)
                into_row, into_col = pieces_of(s, r, c)
                rows.append(r)
                cols.append(c)
                lives.append(jnp.where(s < count_ref[0], 1.0, 0.0).astype(F32))
                into_rows.append(into_row)
                into_cols.append(into_col)
            for size, acc, places, pieces in (
                (col_size, sum_rows, rows, into_rows),
                (grp_size, sum_cols, cols, into_cols),
            ):
                for place in range(size):
                    total = acc[place]
                    for u in range(group):
                        total = total + jnp.where(places[u] == place, lives[u], 0.0) * pieces[u]
                    acc[place] = total
            return carry

        lax.fori_loop(0, slots // group, visit, 0)

    ones = jnp.ones((width, tile_size), BF16)

    def degree_pieces(s, r, c):
        load_tile(s).wait()
        first, second = split_two(raw[s])
        high[s] = first
        low[s] = second
        into_row = dot_nt(ones, first) + dot_nt(ones, second)
        into_col = dot_nn(ones, first) + dot_nn(ones, second)
        return into_row, into_col

    def product_pieces(s, r, c):
        first, second = high[s], low[s]
        at_col, at_row = col_split[c], row_split[r]
        into_row = dot_nt(at_col, first)
        into_row = into_row[:width] + into_row[width:] + dot_nt(at_col[:width], second)
        into_col = dot_nn(at_row, first)
        into_col = into_col[:width] + into_col[width:] + dot_nn(at_row[:width], second)
        return into_row, into_col

    degree_refs = (deg_row, deg_col, deg_got_row, deg_got_col)
    product_refs = (acc_row, acc_col, got_row, got_col)
    degree_sems = (deg_row_sem, deg_col_sem)
    product_sems = (scatter_row_sem, scatter_col_sem)

    def next_block(k, gram):
        factor, inverse = factorize(gram)
        factors_ref[k] = factor
        q_ref[k] = dot_nn(inverse, r_ref[...], HIGHEST)
        return inverse

    q_ref[...] = jnp.zeros_like(q_ref)
    proj_ref[...] = jnp.zeros_like(proj_ref)
    r_ref[...] = start_ref[...]
    start_part = gram_part(start_ref[...])
    pl.semaphore_wait(barrier, col_size + grp_size - 2)
    reduce_start(start_part, two_col, two_col_sem)
    gather(True)
    add_tiles(degree_pieces, deg_row, deg_col)
    scatter(*degree_refs, *degree_sems, True)

    def step(k, carry):
        newest = r_ref[...]
        row_panel[col] = newest
        col_panel[grp] = newest
        gather(False)
        for size, panel, halves in (
            (grp_size, col_panel, col_split),
            (col_size, row_panel, row_split),
        ):
            for place in range(size):
                first, second = split_two(panel[place])
                halves[place, :width] = first
                halves[place, width:] = second
        add_tiles(product_pieces, acc_row, acc_col)
        scatter(*product_refs, *product_sems, True)
        reduce_turn(two_col, two_grp, two_col_sem, two_grp_sem)

        @pl.when(k == 0)
        def _():
            scatter(*degree_refs, *degree_sems, False)
            degree_ref[...] = total_of(*degree_refs)

        inverse = next_block(k, reduce_end(two_grp, two_grp_sem))
        scatter(*product_refs, *product_sems, False)
        laplace = degree_ref[...] * newest - total_of(*product_refs)
        applied = dot_nn(inverse, laplace, HIGHEST)
        stacked = q_ref[...].reshape(-1, tile_size)
        reduce_start(dot_nt(applied, stacked, HIGHEST), one_col, one_col_sem)
        reduce_turn(one_col, one_grp, one_col_sem, one_grp_sem)
        coeffs = reduce_end(one_grp, one_grp_sem)
        for j in range(ITERS):
            proj_ref[k, j] = coeffs[:, j * width : (j + 1) * width]
        residual = applied - dot_nn(coeffs, stacked, HIGHEST)
        r_ref[...] = residual

        @pl.when(k < ITERS - 1)
        def _():
            gather(True)

        reduce_start(gram_part(residual), two_col, two_col_sem)
        return carry

    lax.fori_loop(0, ITERS, step, 0)
    reduce_turn(two_col, two_grp, two_col_sem, two_grp_sem)
    next_block(ITERS, reduce_end(two_grp, two_grp_sem))
    basis_ref[...] = q_ref[: ITERS + 1]


def solution(mesh):
    grp_size, col_size = mesh.shape["grp"], mesh.shape["col"]

    def body(start_block, tile_values, tile_row, tile_col, tile_count):
        width, shard_len = start_block.shape
        slots, tile_size = tile_values.shape[2], tile_values.shape[3]
        assert shard_len == tile_size and LANES % width == 0
        places = LANES // width
        node_total = shard_len * grp_size * col_size
        vmem = pl.BlockSpec(memory_space=pltpu.VMEM)
        smem = pl.BlockSpec(memory_space=pltpu.SMEM)
        block = (width, tile_size)
        small = (width, LANES)

        def sems(size):
            return pltpu.SemaphoreType.DMA((2, size))

        return pl.pallas_call(
            functools.partial(kernel, grp_size, col_size, node_total),
            out_shape=(
                jax.ShapeDtypeStruct((ITERS + 1,) + block, F32),
                jax.ShapeDtypeStruct((ITERS, ITERS, width, width), F32),
                jax.ShapeDtypeStruct((ITERS + 1, width, width), F32),
            ),
            in_specs=[vmem, pl.BlockSpec(memory_space=pl.ANY), smem, smem, smem],
            out_specs=(vmem, vmem, vmem),
            scratch_shapes=[
                pltpu.VMEM((slots, tile_size, tile_size), F32),
                pltpu.VMEM((slots, tile_size, tile_size), BF16),
                pltpu.VMEM((slots, tile_size, tile_size), BF16),
                pltpu.VMEM((places,) + block, F32),
                pltpu.VMEM((col_size,) + block, F32),
                pltpu.VMEM((grp_size,) + block, F32),
                pltpu.VMEM((col_size, 2 * width, tile_size), BF16),
                pltpu.VMEM((grp_size, 2 * width, tile_size), BF16),
                pltpu.VMEM((col_size,) + block, F32),
                pltpu.VMEM((grp_size,) + block, F32),
                pltpu.VMEM((col_size,) + block, F32),
                pltpu.VMEM((grp_size,) + block, F32),
                pltpu.VMEM((col_size,) + block, F32),
                pltpu.VMEM((grp_size,) + block, F32),
                pltpu.VMEM((col_size,) + block, F32),
                pltpu.VMEM((grp_size,) + block, F32),
                pltpu.VMEM(block, F32),
                pltpu.VMEM(block, F32),
                pltpu.VMEM((col_size,) + small, F32),
                pltpu.VMEM((grp_size,) + small, F32),
                pltpu.VMEM((col_size,) + small, F32),
                pltpu.VMEM((grp_size,) + small, F32),
                pltpu.SemaphoreType.DMA((slots,)),
                sems(col_size), sems(grp_size), sems(col_size), sems(grp_size),
                sems(col_size), sems(grp_size),
                sems(col_size), sems(grp_size), sems(col_size), sems(grp_size),
            ],
            compiler_params=pltpu.CompilerParams(
                collective_id=0, has_side_effects=True, vmem_limit_bytes=40 * 1024 * 1024
            ),
        )(
            start_block,
            tile_values.reshape(slots, tile_size, tile_size),
            tile_row.reshape(slots),
            tile_col.reshape(slots),
            tile_count.reshape(1),
        )

    in_specs = (
        P(None, ("grp", "col")),
        P("grp", "col", None, None, None),
        P("grp", "col", None),
        P("grp", "col", None),
        P("grp", "col"),
    )
    out_specs = (P(None, None, ("grp", "col")), P(), P())
    return jax.shard_map(body, mesh=mesh, in_specs=in_specs, out_specs=out_specs, check_vma=False)
```

```python
import functools

import jax
import jax.numpy as jnp
from jax import lax
from jax.experimental import pallas as pl
from jax.experimental.pallas import tpu as pltpu
from jax.sharding import PartitionSpec as P

ITERS = 4
HIGHEST = lax.Precision.HIGHEST
MESH = pl.DeviceIdType.MESH
F32 = jnp.float32
BF16 = jnp.bfloat16
LANES = 128


def dot_nt(left, right, precision=None):
    dims = (((1,), (1,)), ((), ()))
    return lax.dot_general(left, right, dims, precision=precision, preferred_element_type=F32)


def dot_nn(left, right, precision=None):
    dims = (((1,), (0,)), ((), ()))
    return lax.dot_general(left, right, dims, precision=precision, preferred_element_type=F32)


def split_two(value):
    high = value.astype(BF16)
    low = (value - high.astype(F32)).astype(BF16)
    return high, low


def factorize(gram):
    width = gram.shape[0]
    row = lax.broadcasted_iota(jnp.int32, gram.shape, 0)
    lane = lax.broadcasted_iota(jnp.int32, gram.shape, 1)
    unit = jnp.where(lane == row + width, 1.0, 0.0).astype(F32)
    work = jnp.where(lane < width, gram, unit)
    for j in range(width):
        column = jnp.broadcast_to(work[:, j : j + 1], work.shape)
        pivot_row = jnp.broadcast_to(work[j : j + 1, :], work.shape)
        pivot = jnp.broadcast_to(column[j : j + 1, :], work.shape)
        scale = jnp.where(row > j, column / pivot, 0.0)
        work = work - scale * pivot_row
    diagonal = jnp.sum(jnp.where(lane == row, work, 0.0), axis=1, keepdims=True)
    work = work / jnp.sqrt(diagonal)
    upper = jnp.where((lane < width) & (lane >= row), work, 0.0)
    identity = jnp.where(lane == row, 1.0, 0.0).astype(F32)
    factor = dot_nt(identity, jnp.concatenate([upper] * (LANES // width), axis=0), HIGHEST)
    return factor[:, :width], work[:, width : 2 * width]


def kernel(
    grp_size, col_size, node_total,
    start_ref, tiles_ref, row_ref, col_ref, count_ref,
    basis_ref, proj_ref, factors_ref,
    raw, high, low, q_ref, row_panel, col_panel, row_split, col_split,
    acc_row, acc_col, got_row, got_col, deg_row, deg_col, deg_got_row, deg_got_col,
    degree_ref, r_ref, one_col, one_grp, two_col, two_grp,
    tile_sem, gather_row_sem, gather_col_sem, scatter_row_sem, scatter_col_sem,
    deg_row_sem, deg_col_sem,
    one_col_sem, one_grp_sem, two_col_sem, two_grp_sem,
):
    grp = lax.axis_index("grp")
    col = lax.axis_index("col")
    slots, tile_size = raw.shape[0], raw.shape[1]
    width = start_ref.shape[0]
    group = 4 if slots % 4 == 0 else 1

    def load_tile(s):
        return pltpu.make_async_copy(tiles_ref.at[s], raw.at[s], tile_sem.at[s])

    def start_load(s, carry):
        load_tile(s).start()
        return carry

    lax.fori_loop(0, slots, start_load, 0)

    barrier = pltpu.get_barrier_semaphore()

    def greet_col(d, carry):
        pl.semaphore_signal(
            barrier, inc=1, device_id=(grp, lax.rem(col + d, col_size)), device_id_type=MESH
        )
        return carry

    def greet_grp(d, carry):
        pl.semaphore_signal(
            barrier, inc=1, device_id=(lax.rem(grp + d, grp_size), col), device_id_type=MESH
        )
        return carry

    lax.fori_loop(1, col_size, greet_col, 0)
    lax.fori_loop(1, grp_size, greet_grp, 0)

    def exchange(axis, source, target, sems, start):
        size = col_size if axis == "col" else grp_size
        me = col if axis == "col" else grp

        def visit(d, carry):
            peer = lax.rem(me + d, size)
            copy = pltpu.make_async_remote_copy(
                src_ref=source(peer),
                dst_ref=target,
                send_sem=sems.at[0, d],
                recv_sem=sems.at[1, d],
                device_id=(grp, peer) if axis == "col" else (peer, col),
                device_id_type=MESH,
            )
            if start:
                copy.start()
            else:
                copy.wait()
            return carry

        lax.fori_loop(1, size, visit, 0, unroll=size <= 8)

    def reduce_start(part, col_buf, col_sems):
        col_buf[col] = part
        exchange("col", lambda peer: col_buf.at[col], col_buf.at[col], col_sems, True)

    def reduce_turn(col_buf, grp_buf, col_sems, grp_sems):
        exchange("col", lambda peer: col_buf.at[col], col_buf.at[col], col_sems, False)
        grp_buf[grp] = jnp.sum(col_buf[...], axis=0)
        exchange("grp", lambda peer: grp_buf.at[grp], grp_buf.at[grp], grp_sems, True)

    def reduce_end(grp_buf, grp_sems):
        exchange("grp", lambda peer: grp_buf.at[grp], grp_buf.at[grp], grp_sems, False)
        return jnp.sum(grp_buf[...], axis=0) / node_total

    def gram_part(block):
        return dot_nt(block, jnp.concatenate([block] * (LANES // width), axis=0), HIGHEST)

    def scatter(rows, cols, row_in, col_in, row_sems, col_sems, start):
        exchange("col", lambda peer: rows.at[peer], row_in.at[col], row_sems, start)
        exchange("grp", lambda peer: cols.at[peer], col_in.at[grp], col_sems, start)

    def total_of(rows, cols, row_in, col_in):
        row_in[col] = rows[col]
        col_in[grp] = cols[grp]
        return jnp.sum(row_in[...], axis=0) + jnp.sum(col_in[...], axis=0)

    def gather(start):
        exchange("col", lambda peer: r_ref, row_panel.at[col], gather_row_sem, start)
        exchange("grp", lambda peer: r_ref, col_panel.at[grp], gather_col_sem, start)

    def add_tiles(pieces_of, sum_rows, sum_cols):
        sum_rows[...] = jnp.zeros_like(sum_rows)
        sum_cols[...] = jnp.zeros_like(sum_cols)

        def visit(n, carry):
            rows, cols, into_rows, into_cols, lives = [], [], [], [], []
            for u in range(group):
                s = n * group + u
                r = jnp.clip(row_ref[s] - grp * col_size, 0, col_size - 1)
                c = jnp.clip(lax.div(col_ref[s], col_size), 0, grp_size - 1)
                into_row, into_col = pieces_of(s, r, c)
                rows.append(r)
                cols.append(c)
                lives.append(jnp.where(s < count_ref[0], 1.0, 0.0).astype(F32))
                into_rows.append(into_row)
                into_cols.append(into_col)
            for size, acc, places, pieces in (
                (col_size, sum_rows, rows, into_rows),
                (grp_size, sum_cols, cols, into_cols),
            ):
                for place in range(size):
                    total = acc[place]
                    for u in range(group):
                        total = total + jnp.where(places[u] == place, lives[u], 0.0) * pieces[u]
                    acc[place] = total
            return carry

        lax.fori_loop(0, slots // group, visit, 0)

    ones = jnp.ones((width, tile_size), BF16)

    def degree_pieces(s, r, c):
        load_tile(s).wait()
        first, second = split_two(raw[s])
        high[s] = first
        low[s] = second
        into_row = dot_nt(ones, first) + dot_nt(ones, second)
        into_col = dot_nn(ones, first) + dot_nn(ones, second)
        return into_row, into_col

    def product_pieces(s, r, c):
        first, second = high[s], low[s]
        at_col, at_row = col_split[c], row_split[r]
        into_row = dot_nt(at_col, first)
        into_row = into_row[:width] + into_row[width:] + dot_nt(at_col[:width], second)
        into_col = dot_nn(at_row, first)
        into_col = into_col[:width] + into_col[width:] + dot_nn(at_row[:width], second)
        return into_row, into_col

    degree_refs = (deg_row, deg_col, deg_got_row, deg_got_col)
    product_refs = (acc_row, acc_col, got_row, got_col)
    degree_sems = (deg_row_sem, deg_col_sem)
    product_sems = (scatter_row_sem, scatter_col_sem)

    def next_block(k, gram):
        factor, inverse = factorize(gram)
        factors_ref[k] = factor
        q_ref[k] = dot_nn(inverse, r_ref[...], HIGHEST)
        return inverse

    q_ref[...] = jnp.zeros_like(q_ref)
    proj_ref[...] = jnp.zeros_like(proj_ref)
    r_ref[...] = start_ref[...]
    start_part = gram_part(start_ref[...])
    pl.semaphore_wait(barrier, col_size + grp_size - 2)
    reduce_start(start_part, two_col, two_col_sem)
    gather(True)
    add_tiles(degree_pieces, deg_row, deg_col)
    scatter(*degree_refs, *degree_sems, True)

    def step(k, carry):
        newest = r_ref[...]
        row_panel[col] = newest
        col_panel[grp] = newest
        gather(False)
        for size, panel, halves in (
            (grp_size, col_panel, col_split),
            (col_size, row_panel, row_split),
        ):
            for place in range(size):
                first, second = split_two(panel[place])
                halves[place, :width] = first
                halves[place, width:] = second
        reduce_turn(two_col, two_grp, two_col_sem, two_grp_sem)
        add_tiles(product_pieces, acc_row, acc_col)
        scatter(*product_refs, *product_sems, True)

        @pl.when(k == 0)
        def _():
            scatter(*degree_refs, *degree_sems, False)
            degree_ref[...] = total_of(*degree_refs)

        inverse = next_block(k, reduce_end(two_grp, two_grp_sem))
        scatter(*product_refs, *product_sems, False)
        laplace = degree_ref[...] * newest - total_of(*product_refs)
        applied = dot_nn(inverse, laplace, HIGHEST)
        stacked = q_ref[...].reshape(-1, tile_size)
        reduce_start(dot_nt(applied, stacked, HIGHEST), one_col, one_col_sem)
        reduce_turn(one_col, one_grp, one_col_sem, one_grp_sem)
        coeffs = reduce_end(one_grp, one_grp_sem)
        residual = applied - dot_nn(coeffs, stacked, HIGHEST)
        r_ref[...] = residual

        @pl.when(k < ITERS - 1)
        def _():
            gather(True)

        reduce_start(gram_part(residual), two_col, two_col_sem)
        for j in range(ITERS):
            proj_ref[k, j] = coeffs[:, j * width : (j + 1) * width]
        return carry

    lax.fori_loop(0, ITERS, step, 0)
    reduce_turn(two_col, two_grp, two_col_sem, two_grp_sem)
    next_block(ITERS, reduce_end(two_grp, two_grp_sem))
    basis_ref[...] = q_ref[: ITERS + 1]


def solution(mesh):
    grp_size, col_size = mesh.shape["grp"], mesh.shape["col"]

    def body(start_block, tile_values, tile_row, tile_col, tile_count):
        width, shard_len = start_block.shape
        slots, tile_size = tile_values.shape[2], tile_values.shape[3]
        assert shard_len == tile_size and LANES % width == 0
        places = LANES // width
        node_total = shard_len * grp_size * col_size
        vmem = pl.BlockSpec(memory_space=pltpu.VMEM)
        smem = pl.BlockSpec(memory_space=pltpu.SMEM)
        block = (width, tile_size)
        small = (width, LANES)

        def sems(size):
            return pltpu.SemaphoreType.DMA((2, size))

        return pl.pallas_call(
            functools.partial(kernel, grp_size, col_size, node_total),
            out_shape=(
                jax.ShapeDtypeStruct((ITERS + 1,) + block, F32),
                jax.ShapeDtypeStruct((ITERS, ITERS, width, width), F32),
                jax.ShapeDtypeStruct((ITERS + 1, width, width), F32),
            ),
            in_specs=[vmem, pl.BlockSpec(memory_space=pl.ANY), smem, smem, smem],
            out_specs=(vmem, vmem, vmem),
            scratch_shapes=[
                pltpu.VMEM((slots, tile_size, tile_size), F32),
                pltpu.VMEM((slots, tile_size, tile_size), BF16),
                pltpu.VMEM((slots, tile_size, tile_size), BF16),
                pltpu.VMEM((places,) + block, F32),
                pltpu.VMEM((col_size,) + block, F32),
                pltpu.VMEM((grp_size,) + block, F32),
                pltpu.VMEM((col_size, 2 * width, tile_size), BF16),
                pltpu.VMEM((grp_size, 2 * width, tile_size), BF16),
                pltpu.VMEM((col_size,) + block, F32),
                pltpu.VMEM((grp_size,) + block, F32),
                pltpu.VMEM((col_size,) + block, F32),
                pltpu.VMEM((grp_size,) + block, F32),
                pltpu.VMEM((col_size,) + block, F32),
                pltpu.VMEM((grp_size,) + block, F32),
                pltpu.VMEM((col_size,) + block, F32),
                pltpu.VMEM((grp_size,) + block, F32),
                pltpu.VMEM(block, F32),
                pltpu.VMEM(block, F32),
                pltpu.VMEM((col_size,) + small, F32),
                pltpu.VMEM((grp_size,) + small, F32),
                pltpu.VMEM((col_size,) + small, F32),
                pltpu.VMEM((grp_size,) + small, F32),
                pltpu.SemaphoreType.DMA((slots,)),
                sems(col_size), sems(grp_size), sems(col_size), sems(grp_size),
                sems(col_size), sems(grp_size),
                sems(col_size), sems(grp_size), sems(col_size), sems(grp_size),
            ],
            compiler_params=pltpu.CompilerParams(
                collective_id=0, has_side_effects=True, vmem_limit_bytes=40 * 1024 * 1024
            ),
        )(
            start_block,
            tile_values.reshape(slots, tile_size, tile_size),
            tile_row.reshape(slots),
            tile_col.reshape(slots),
            tile_count.reshape(1),
        )

    in_specs = (
        P(None, ("grp", "col")),
        P("grp", "col", None, None, None),
        P("grp", "col", None),
        P("grp", "col", None),
        P("grp", "col"),
    )
    out_specs = (P(None, None, ("grp", "col")), P(), P())
    return jax.shard_map(body, mesh=mesh, in_specs=in_specs, out_specs=out_specs, check_vma=False)
```
